32 devices in a mesh: tm: 8 (over z, x), freq: 4 (over y, core).
Axes of the slice: x: 2, y: 2, z: 4, core: 2. Of those that a mesh axis runs over, the one named last changes fastest.
Arguments:
- waveform: float32 [1048576], P(('tm', 'freq')), may hold values from -24.5 to 24.5
- starts: int32 [4096], P(('tm', 'freq')), may hold values from 0 to 1048575, as said below
- templates: float32 [1024, 512], P('freq'), may hold values from 0.05 to 2
- activations: float32 [4096, 512], P('tm', 'freq'), may hold values from 0.05 to 2
Outputs:
- templates_out: float32 [1024, 512], P('freq')
- activations_out: float32 [4096, 512], P('tm', 'freq')
The draws below stay inside these ranges and needn't reach their ends.
Inputs may be any that keep to these rules, and one draw needn't show every extreme that they name: Frame j starts within the stretch of 32768 samples numbered j // 128: (j // 128) * 32768 <= starts[j] < (j // 128 + 1) * 32768.
All inputs are finite; a program needn't handle non-finite values.
Results may differ from the reference program's by a relative error of at most 0.003.
The reference program's roundings to bfloat16 on the way (of `frames`, `fourier` and `ratios`) count: a program that leaves them out, or rounds other values in their place, can miss the bound.
Values may be sent and summed in bfloat16 or wider, within the bound.
No kernel may reach another device: no remote copies, remote signals or barrier semaphores. Data moves between devices by JAX's collectives and lax.ppermute only.
A program may use at most 64 MiB of HBM per device.

```python
import math
import jax
import jax.numpy as jnp
from jax import lax

FLEN = 2048
BINS = 1024
K = 512
ITERS = 2
FR_DEV = 128
SEG = 32768
FRAMES = 4096
SAMPLES = 1048576


def draw_starts(key, part):
    block_count = FRAMES // FR_DEV
    inside_starts = jax.random.randint(jax.random.fold_in(key, 11), (block_count, FR_DEV), 0, SEG)
    edge_starts = jax.random.randint(jax.random.fold_in(key, 12), (block_count, 1), SEG - FLEN + 1, SEG)
    edge_column = jax.random.randint(jax.random.fold_in(key, 13), (block_count, 1), 0, FR_DEV)
    chosen = jnp.where(jnp.arange(FR_DEV)[None, :] == edge_column, edge_starts, inside_starts)
    return (chosen + jnp.arange(block_count)[:, None] * SEG).reshape(FRAMES).astype(jnp.int32)


def draw_waveform(key, part):
    spacing = FLEN // 4
    blocks = SAMPLES // spacing + 1
    place = jax.random.randint(jax.random.fold_in(key, 21), (blocks,), 0, spacing)
    sign_bits = jax.random.randint(jax.random.fold_in(key, 22), (blocks,), 0, 2)
    signs = sign_bits.astype(jnp.float32) * 2.0 - 1.0
    magnitude = jax.random.uniform(jax.random.fold_in(key, 23), (blocks,), jnp.float32, 8.0, 24.0)
    background = jnp.clip(0.05 * jax.random.normal(jax.random.fold_in(key, 24), (blocks * spacing,), jnp.float32), -0.25, 0.25)
    spikes = jnp.where(jnp.arange(spacing)[None, :] == place[:, None], (signs * magnitude)[:, None], 0.0)
    return (spikes.reshape(-1) + background)[:SAMPLES].astype(jnp.float32)


def block_scale(stream_key, dims, shards, low, largest):
    def one(position, blocks):
        steps = jax.random.uniform(jax.random.fold_in(jax.random.fold_in(stream_key, 6), position), (blocks,), jnp.float32, low / len(shards), largest / len(shards))
        return jnp.repeat(jnp.exp(steps), dims[position] // blocks).reshape((-1,) + (1,) * (len(dims) - position - 1))

    gain = one(*shards[0])
    for cut in shards[1:]:
        gain = gain * one(*cut)
    return gain


def setup_inputs(seed: int = 0) -> dict:
    splits = jax.random.split(jax.random.key(seed), 5)
    waveform = draw_waveform(jax.random.fold_in(splits[4], 71), 0)
    starts = draw_starts(jax.random.fold_in(splits[4], 71), 0)
    templates = jnp.clip(jnp.exp(math.log(2.0) - 3.6888794 * jax.random.uniform(splits[2], (BINS, K), jnp.float32) ** block_scale(splits[2], (BINS, K), ((0, 4),), -0.2, 0.2)), 0.05, 2.0)
    activations = jnp.clip(jnp.exp(math.log(2.0) - 3.6888794 * jax.random.uniform(splits[3], (FRAMES, K), jnp.float32) ** block_scale(splits[3], (FRAMES, K), ((0, 8), (1, 4)), -0.2, 0.2)), 0.05, 2.0)
    return {"waveform": waveform, "starts": starts, "templates": templates, "activations": activations}


def fourier_table(length, bins):
    row_index = jnp.arange(length, dtype=jnp.int32)[:, None]
    bin_index = jnp.arange(bins, dtype=jnp.int32)[None, :]
    phase = ((row_index * bin_index) % length).astype(jnp.float32) * (2.0 * math.pi / length)
    return jnp.concatenate([jnp.cos(phase), -jnp.sin(phase)], axis=1).astype(jnp.bfloat16)


def hann_window(length):
    steps_all = jnp.arange(length, dtype=jnp.int32).astype(jnp.float32)
    return 0.5 - 0.5 * jnp.cos(steps_all * (2.0 * math.pi / length))


def reference(waveform, starts, templates, activations):
    fourier = fourier_table(FLEN, BINS)
    window = hann_window(FLEN)
    padded = jnp.concatenate([waveform, jnp.zeros((FLEN,), waveform.dtype)])

    def one_block(block_starts):
        frames = jax.vmap(lambda offset: lax.dynamic_slice(padded, (offset,), (FLEN,)))(block_starts)
        frames = (frames * window[None, :]).astype(jnp.bfloat16)
        spectrum = jnp.dot(frames, fourier, preferred_element_type=jnp.float32)
        return (spectrum[:, :BINS] ** 2 + spectrum[:, BINS:] ** 2) * 0.25

    energy = lax.map(one_block, starts.reshape(-1, FR_DEV)).reshape(FRAMES, BINS)
    weights_now = templates
    acts_now = activations
    for iteration in range(ITERS):
        templates_half = weights_now.astype(jnp.bfloat16)
        acts_half = acts_now.astype(jnp.bfloat16)
        rebuilt = lax.dot_general(acts_half, templates_half, (((1,), (1,)), ((), ())), preferred_element_type=jnp.float32)
        ratios = (energy / rebuilt).astype(jnp.bfloat16)
        numerator = jnp.dot(ratios, templates_half, preferred_element_type=jnp.float32)
        template_mass = jnp.sum(weights_now, axis=0)
        acts_now = acts_now * numerator / template_mass[None, :]
        acts_half = acts_now.astype(jnp.bfloat16)
        rebuilt = lax.dot_general(acts_half, templates_half, (((1,), (1,)), ((), ())), preferred_element_type=jnp.float32)
        ratios = (energy / rebuilt).astype(jnp.bfloat16)
        template_numerator = lax.dot_general(ratios, acts_half, (((0,), (0,)), ((), ())), preferred_element_type=jnp.float32)
        column_totals = jnp.sum(acts_half.astype(jnp.float32), axis=0)
        weights_now = weights_now * template_numerator / column_totals[None, :]
    return weights_now, acts_now
```

```python
import functools
import math

import jax
import jax.numpy as jnp
import numpy as np
from jax import lax
from jax.experimental import pallas as pl
from jax.experimental.pallas import tpu as pltpu
from jax.sharding import PartitionSpec as P

ITERS = 2
LANES = 128
AUX = 16
BF16 = jnp.bfloat16
F32 = jnp.float32
VMEM = pl.BlockSpec(memory_space=pltpu.VMEM)
SMEM = pl.BlockSpec(memory_space=pltpu.SMEM)

NT = (((1,), (1,)), ((), ()))
NN = (((1,), (0,)), ((), ()))


def dot(a, b, dims=NN):
    return lax.dot_general(a, b, dims, preferred_element_type=F32)


def split_rows(total):
    high = total.astype(BF16)
    low = (total - high.astype(F32)).astype(BF16)
    row = lax.broadcasted_iota(jnp.int32, (AUX, total.shape[1]), 0)
    rows = jnp.where(row == 0, high.astype(F32), jnp.where(row == 1, low.astype(F32), 0.0))
    return rows.astype(BF16)


def join_rows(block):
    both = block.astype(F32)
    return both[0:1, :] + both[1:2, :]


def call(body, name, out_shape, *args, in_specs=None, scratch=(), flops=0, nbytes=1 << 20):
    return pl.pallas_call(
        body,
        out_shape=out_shape,
        in_specs=in_specs if in_specs is not None else [VMEM] * len(args),
        out_specs=jax.tree.map(lambda _: VMEM, out_shape),
        scratch_shapes=list(scratch),
        name=name,
        cost_estimate=pl.CostEstimate(flops=flops, bytes_accessed=nbytes, transcendentals=0),
        compiler_params=pltpu.CompilerParams(vmem_limit_bytes=40 << 20),
    )(*args)


def shape(rows, cols, dtype):
    return jax.ShapeDtypeStruct((rows, cols), dtype)


def angle_tables(length, bins, step):
    k = np.arange(bins)[None, :]

    def angles(n):
        return (n[:, None] * k % length) * (2.0 * math.pi / length)

    coarse = angles(np.arange(length // 2 // step) * step)
    fine = angles(np.arange(step))
    return np.concatenate([np.cos(coarse), np.sin(coarse), np.cos(fine), np.sin(fine)]).astype(np.float32)


def hann_rows(length):
    window = 0.5 - 0.5 * np.cos(np.arange(length) * (2.0 * math.pi / length))
    return window.astype(np.float32).reshape(length // LANES, LANES)


def pack_inputs(w_ref, a_ref, out_ref):
    bins, width = w_ref.shape
    part = a_ref.shape[0] // 4
    own = a_ref.shape[1]
    w = w_ref[...]
    out_ref[0:bins, 0:width] = w.astype(BF16)
    out_ref[bins : bins + AUX, 0:width] = split_rows(jnp.sum(w, axis=0, keepdims=True))
    out_ref[bins : bins + AUX, width:] = jnp.zeros((AUX, 4 * own), BF16)
    for core in range(2):
        for side in range(2):
            a = a_ref[(2 * side + core) * part : (2 * side + core + 1) * part, :]
            high = a.astype(BF16)
            low = (a - high.astype(F32)).astype(BF16)
            rows = slice(side * part, (side + 1) * part)
            out_ref[rows, width + core * own : width + (core + 1) * own] = high
            out_ref[rows, width + (2 + core) * own : width + (3 + core) * own] = low


def build_table(where_ref, base_ref, out_ref, *, step, block, half):
    coarse = out_ref.shape[0] // step
    place = where_ref[0]
    xbit = where_ref[1]
    for turn in range(4):
        for side in range(2):
            start = (place ^ turn) * block + (xbit ^ side) * half
            cols = pl.ds(pl.multiple_of(start, LANES), half)
            c2 = base_ref[2 * coarse : 2 * coarse + step, cols]
            s2 = base_ref[2 * coarse + step : 2 * coarse + 2 * step, cols]
            cos_at = slice(turn * 2 * block + side * half, turn * 2 * block + (side + 1) * half)
            sin_at = slice(cos_at.start + block, cos_at.stop + block)
            for n in range(coarse):
                c1 = base_ref[n : n + 1, cols]
                s1 = base_ref[coarse + n : coarse + n + 1, cols]
                rows = slice(n * step, (n + 1) * step)
                out_ref[rows, cos_at] = (c1 * c2 - s1 * s2).astype(BF16)
                out_ref[rows, sin_at] = (-(s1 * c2 + c1 * s2)).astype(BF16)


def spectrogram(
    where_ref, own_starts, side_starts, own_wave, own_rim, side_wave, side_rim, window_ref, table_ref,
    energy_ref, turned_ref, ext_ref, raw_ref, frames_ref, *, segment,
):
    tiles = window_ref.shape[0]
    length = tiles * LANES
    per = own_starts.shape[0]
    count = 2 * per
    wave_rows = own_wave.shape[0]
    place = where_ref[0]
    side = lax.shift_right_logical(place, 1)
    for index, (wave, rim) in enumerate(((own_wave, own_rim), (side_wave, side_rim))):
        ext_ref[index, 0:wave_rows, :] = wave[...]
        ext_ref[index, wave_rows : wave_rows + tiles, :] = rim[...]
    lane = lax.broadcasted_iota(jnp.int32, (tiles, LANES), 1)
    window = window_ref[...]

    def one(index, starts, slot, i):
        if segment & (segment - 1) == 0:
            start = starts[i] & (segment - 1)
        else:
            start = lax.rem(starts[i], segment)
        row = lax.shift_right_logical(start, 7)
        shift = start & (LANES - 1)
        back = (LANES - shift) & (LANES - 1)
        first = ext_ref[index, pl.ds(row, tiles), :]
        second = ext_ref[index, pl.ds(row + 1, tiles), :]
        first = pltpu.roll(first, back, 1)
        second = pltpu.roll(second, back, 1)
        frame = jnp.where(lane < LANES - shift, first, second) * window
        raw_ref[pl.ds(slot * per + i, tiles, stride=count), :] = frame

    def body(i, carry):
        one(0, own_starts, side, i)
        one(1, side_starts, 1 - side, i)
        return carry

    lax.fori_loop(0, per, body, 0, unroll=4)
    half = tiles // 2
    for j in range(tiles):
        rows = slice((j // half) * count, (j // half + 1) * count)
        cols = slice((j % half) * LANES, (j % half + 1) * LANES)
        frames_ref[rows, cols] = raw_ref[j * count : (j + 1) * count, :].astype(BF16)
    block = energy_ref.shape[1] // 4
    parity = lax.broadcasted_iota(jnp.int32, (1, 2 * block), 1) & 1
    sign = 1.0 - 2.0 * parity.astype(F32)
    for turn in range(4):
        both = dot(frames_ref[...], table_ref[:, turn * 2 * block : (turn + 1) * 2 * block])
        whole = both[:count] + sign * both[count:]
        energy = (whole[:, :block] ** 2 + whole[:, block:] ** 2) * 0.25
        energy_ref[:, turn * block : (turn + 1) * block] = energy
        if turn < 2:
            turned_ref[turn * block : (turn + 1) * block, :] = energy.T


def update_acts(acts, energy_ref, turned_ref, templates, mass, own_ref, send_ref, acts_ref, total_ref):
    block = energy_ref.shape[1] // 4
    half_acts = acts.astype(BF16)
    numerator = None
    for turn in range(4):
        w = templates[turn * block : (turn + 1) * block, :]
        ratios = (energy_ref[:, turn * block : (turn + 1) * block] / dot(half_acts, w, NT)).astype(BF16)
        term = dot(ratios, w)
        numerator = term if numerator is None else numerator + term
    acts = acts * numerator / mass
    acts_ref[...] = acts
    half_acts = acts.astype(BF16)
    total = jnp.sum(half_acts.astype(F32), axis=0, keepdims=True)
    total_ref[...] = jnp.broadcast_to(total, total_ref.shape)
    send_ref[block : block + AUX, :] = split_rows(total)
    for turn in range(2):
        w = templates[turn * block : (turn + 1) * block, :]
        ratios = (turned_ref[turn * block : (turn + 1) * block, :] / dot(w, half_acts, NT)).astype(BF16)
        term = dot(ratios, half_acts)
        if turn == 0:
            own_ref[...] = term
        else:
            send_ref[0:block, :] = term.astype(BF16)


def first_update(where_ref, energy_ref, turned_ref, p0, p1, p2, p3, own_ref, send_ref, acts_ref, total_ref, w_ref, a_ref):
    block = energy_ref.shape[1] // 4
    half = block // 2
    width = w_ref.shape[1]
    quarter = width // 4
    place = where_ref[0]
    xbit = where_ref[1]
    core = place & 1
    mass = None
    for turn, pack in enumerate((p0, p1, p2, p3)):
        for side in range(2):
            rows = pl.ds(pl.multiple_of((xbit ^ side) * half, half), half)
            w_ref[turn * block + side * half : turn * block + (side + 1) * half, :] = pack[rows, 0:width]
        part = join_rows(pack[block : block + AUX, 0:width])
        mass = part if mass is None else mass + part
        high = pack[0 : a_ref.shape[0], pl.ds(pl.multiple_of(width + core * quarter, LANES), quarter)]
        low = pack[0 : a_ref.shape[0], pl.ds(pl.multiple_of(width + (2 + core) * quarter, LANES), quarter)]
        cols = pl.ds(pl.multiple_of((place ^ turn) * quarter, LANES), quarter)
        a_ref[:, cols] = high.astype(F32) + low.astype(F32)
    update_acts(a_ref[...], energy_ref, turned_ref, w_ref, mass, own_ref, send_ref, acts_ref, total_ref)


def later_update(*refs):
    where_ref, energy_ref, turned_ref, a_ref = refs[:4]
    pieces = refs[4:12]
    own_ref, send_ref, acts_ref, total_ref, keep_ref, give_ref, w_ref = refs[12:]
    half = pieces[0].shape[0] - AUX
    quarter = keep_ref.shape[1]
    place = where_ref[0]
    mass = None
    for index, piece in enumerate(pieces):
        w_ref[index * half : (index + 1) * half, :] = piece[0:half, :]
        part = join_rows(piece[half : half + AUX, :])
        mass = part if mass is None else mass + part
    update_acts(a_ref[...], energy_ref, turned_ref, w_ref, mass, own_ref, send_ref, acts_ref, total_ref)
    keep_ref[...] = acts_ref[:, pl.ds(pl.multiple_of(place * quarter, LANES), quarter)]
    give_ref[...] = acts_ref[:, pl.ds(pl.multiple_of((place ^ 1) * quarter, LANES), quarter)]


def add_core(own_ref, total_ref, got_ref, keep_ref, send_ref):
    block = own_ref.shape[0]
    half = block // 2
    keep_ref[0:half, :] = own_ref[0:half, :] + got_ref[0:half, :].astype(F32)
    send_ref[0:half, :] = (own_ref[half:block, :] + got_ref[half:block, :].astype(F32)).astype(BF16)
    total = total_ref[0:1, :] + join_rows(got_ref[block : block + AUX, :])
    rows = split_rows(total)
    send_ref[half : half + AUX, :] = rows
    keep_ref[half : half + AUX, :] = rows.astype(F32)


def add_half(keep_ref, got_ref, out_ref):
    half = keep_ref.shape[0] - AUX
    out_ref[0:half, :] = (keep_ref[0:half, :].astype(F32) + got_ref[0:half, :].astype(F32)).astype(BF16)
    total = join_rows(keep_ref[half : half + AUX, :]) + join_rows(got_ref[half : half + AUX, :])
    out_ref[half : half + AUX, :] = split_rows(total)


def new_templates(old, mine_ref, got_ref):
    half = mine_ref.shape[0] - AUX
    numerator = mine_ref[0:half, :].astype(F32) + got_ref[0:half, :].astype(F32)
    total = join_rows(mine_ref[half : half + AUX, :]) + join_rows(got_ref[half : half + AUX, :])
    return old * numerator / total


def first_templates(where_ref, w_ref, mine_ref, got_ref, new_ref, send_ref):
    half = new_ref.shape[0]
    old = w_ref[pl.ds(pl.multiple_of(where_ref[1] * half, half), half), :]
    new = new_templates(old, mine_ref, got_ref)
    new_ref[...] = new
    send_ref[0:half, :] = new.astype(BF16)
    send_ref[half : half + AUX, :] = split_rows(jnp.sum(new, axis=0, keepdims=True))


def last_templates(w_ref, mine_ref, got_ref, new_ref):
    new_ref[...] = new_templates(w_ref[...], mine_ref, got_ref)


def place_outputs(where_ref, mine_ref, got_ref, keep_ref, given_ref, w_out, a_out):
    half = mine_ref.shape[0]
    part = keep_ref.shape[0] // 2
    xbit = where_ref[1]
    core = where_ref[0] & 1
    w_out[pl.ds(pl.multiple_of(xbit * half, half), half), :] = mine_ref[...]
    w_out[pl.ds(pl.multiple_of((1 - xbit) * half, half), half), :] = got_ref[...]
    for side in range(2):
        rows = slice(side * part, (side + 1) * part)
        a_out[pl.ds(pl.multiple_of((2 * side + core) * part, part), part), :] = keep_ref[rows, :]
        a_out[pl.ds(pl.multiple_of((2 * side + 1 - core) * part, part), part), :] = given_ref[rows, :]


def swap(block, axis, bit):
    return lax.ppermute(block, axis, [(i, i ^ bit) for i in range(lax.axis_size(axis))])


def shards(waveform, starts, templates, activations):
    tm, freq = lax.axis_size("tm"), lax.axis_size("freq")
    block, width = templates.shape
    half = block // 2
    count = activations.shape[0] // 2
    bins = block * freq
    segment = waveform.shape[0]
    per = starts.shape[0]
    quarter = activations.shape[1]
    length = 2048
    tiles = length // LANES
    step = 32
    assert freq == 4 and tm & (tm - 1) == 0

    where = jnp.stack([lax.axis_index("freq"), lax.axis_index("tm") & 1]).astype(jnp.int32)

    wave = waveform.reshape(segment // LANES, LANES)
    head = wave[:tiles]
    devices = tm * freq
    own_rim = lax.ppermute(head, ("tm", "freq"), [(i, i - 1) for i in range(1, devices)])
    side_rim = lax.ppermute(head, ("tm", "freq"), [(i, (i - 1) ^ 2) for i in range(1, devices)])
    side_wave = swap(wave, "freq", 2)
    side_starts = swap(starts, "freq", 2)

    pack = call(
        pack_inputs, "pack_inputs", shape(block + AUX, width + 4 * quarter, BF16), templates, activations,
        nbytes=templates.size * 10,
    )
    pack_core = swap(pack, "freq", 1)
    pack_y = swap(pack, "freq", 2)
    pack_both = swap(pack_y, "freq", 1)

    base = jnp.asarray(angle_tables(length, bins, step))
    table = call(
        functools.partial(build_table, step=step, block=block, half=half), "build_table",
        shape(length // 2, 2 * bins, BF16), where, base, in_specs=[SMEM, VMEM], flops=4 << 20, nbytes=8 << 20,
    )
    energy, turned = call(
        functools.partial(spectrogram, segment=segment), "spectrogram",
        (shape(count, bins, F32), shape(2 * block, count, F32)),
        where, starts, side_starts, wave, own_rim, side_wave, side_rim, jnp.asarray(hann_rows(length)), table,
        in_specs=[SMEM, SMEM, SMEM] + [VMEM] * 6,
        scratch=[
            pltpu.VMEM((2, segment // LANES + tiles, LANES), F32),
            pltpu.VMEM((tiles * count, LANES), F32),
            pltpu.VMEM((2 * count, length // 2), BF16),
        ],
        flops=2 * count * length * 2 * bins, nbytes=8 << 20,
    )

    outs = (shape(block, width, F32), shape(block + AUX, width, BF16), shape(count, width, F32), shape(8, width, F32))
    work = 3 * 2 * count * bins * width
    acts = pieces = kept = None
    for iteration in range(ITERS):
        if iteration == 0:
            own, send, acts, total = call(
                first_update, "first_update", outs, where, energy, turned, pack, pack_core, pack_y, pack_both,
                in_specs=[SMEM] + [VMEM] * 6,
                scratch=[pltpu.VMEM((bins, width), BF16), pltpu.VMEM((count, width), F32)], flops=work,
                nbytes=4 << 20,
            )
        else:
            more = (shape(count, quarter, F32), shape(count, quarter, F32))
            own, send, acts, total, keep_acts, give_acts = call(
                later_update, "later_update", outs + more, where, energy, turned, acts, *pieces,
                in_specs=[SMEM] + [VMEM] * 11,
                scratch=[pltpu.VMEM((bins, width), BF16)], flops=work, nbytes=4 << 20,
            )
        got = swap(send, "freq", 1)
        if iteration == ITERS - 1:
            given = swap(give_acts, "freq", 1)
        keep, send = call(
            add_core, "add_core", (shape(half + AUX, width, F32), shape(half + AUX, width, BF16)), own, total, got,
        )
        mine = keep
        got = swap(send, "tm", 1)
        bit = 2
        while bit < tm:
            mine = call(add_half, "add_half", shape(half + AUX, width, BF16), mine, got)
            got = swap(mine, "tm", bit)
            bit *= 2
        if iteration < ITERS - 1:
            kept, send = call(
                first_templates, "first_templates", (shape(half, width, F32), shape(half + AUX, width, BF16)),
                where, templates, mine, got, in_specs=[SMEM] + [VMEM] * 3,
            )
            other = swap(send, "tm", 1)
            in_y = [swap(send, "freq", 2), swap(other, "freq", 2)]
            in_core = [swap(send, "freq", 1), swap(other, "freq", 1)]
            in_both = [swap(in_y[0], "freq", 1), swap(in_y[1], "freq", 1)]
            pieces = [send, other] + in_core + in_y + in_both
        else:
            new = call(last_templates, "last_templates", shape(half, width, F32), kept, mine, got)
            other = swap(new, "tm", 1)
            return tuple(
                call(
                    place_outputs, "place_outputs", (shape(block, width, F32), shape(2 * count, quarter, F32)),
                    where, new, other, keep_acts, given, in_specs=[SMEM] + [VMEM] * 4,
                )
            )


def solution(mesh):
    in_specs = (P(("tm", "freq")), P(("tm", "freq")), P("freq", None), P("tm", "freq"))
    out_specs = (P("freq", None), P("tm", "freq"))
    return jax.shard_map(shards, mesh=mesh, in_specs=in_specs, out_specs=out_specs, check_vma=False)
```

```python
import functools
import math

import jax
import jax.numpy as jnp
import numpy as np
from jax import lax
from jax.experimental import pallas as pl
from jax.experimental.pallas import tpu as pltpu
from jax.sharding import PartitionSpec as P


ITERS = 2
TM, FREQ = "tm", "freq"
LANES = 128
AUX = 16
BF16 = jnp.bfloat16
F32 = jnp.float32
VMEM = pl.BlockSpec(memory_space=pltpu.VMEM)
SMEM = pl.BlockSpec(memory_space=pltpu.SMEM)
HBM = pl.BlockSpec(memory_space=pltpu.HBM)

NT = (((1,), (1,)), ((), ()))
NN = (((1,), (0,)), ((), ()))


def dot(a, b, dims=NN):
    return lax.dot_general(a, b, dims, preferred_element_type=F32)


def split_rows(total):
    high = total.astype(BF16)
    low = (total - high.astype(F32)).astype(BF16)
    row = lax.broadcasted_iota(jnp.int32, (AUX, total.shape[1]), 0)
    rows = jnp.where(row == 0, high.astype(F32), jnp.where(row == 1, low.astype(F32), 0.0))
    return rows.astype(BF16)


def join_rows(block):
    both = block.astype(F32)
    return both[0:1, :] + both[1:2, :]


def stack_lanes(row):
    return jnp.concatenate([row[:, at : at + LANES] for at in range(0, row.shape[1], LANES)], axis=0)


def split_stack(total):
    high = total.astype(BF16).astype(F32)
    rest = jnp.zeros((AUX - 2 * total.shape[0], LANES), F32)
    return jnp.concatenate([high, total - high, rest], axis=0).astype(BF16)


def join_stack(block, lanes):
    both = block.astype(F32)
    return both[0:lanes, :] + both[lanes : 2 * lanes, :]


def call(body, out_shape, *args, in_specs=None, scratch=(), flops=0, nbytes=1 << 20, limit=40 << 20):
    return pl.pallas_call(
        body,
        out_shape=out_shape,
        in_specs=in_specs if in_specs is not None else [VMEM] * len(args),
        out_specs=jax.tree.map(lambda _: VMEM, out_shape),
        scratch_shapes=list(scratch),
        cost_estimate=pl.CostEstimate(flops=flops, bytes_accessed=nbytes, transcendentals=0),
        compiler_params=pltpu.CompilerParams(vmem_limit_bytes=limit),
    )(*args)


def shape(rows, cols, dtype):
    return jax.ShapeDtypeStruct((rows, cols), dtype)


def angle_tables(length, bins, step):
    k = np.arange(bins)[None, :]

    def angles(n):
        return (n[:, None] * k % length) * (2.0 * math.pi / length)

    coarse = angles(np.arange(length // 2 // step) * step)
    fine = angles(np.arange(step))
    return np.concatenate([np.cos(coarse), np.sin(coarse), np.cos(fine), np.sin(fine)]).astype(np.float32)


def hann_rows(length):
    window = 0.5 - 0.5 * np.cos(np.arange(length) * (2.0 * math.pi / length))
    return window.astype(np.float32).reshape(length // LANES, LANES)


def prepare(w_hbm, a_hbm, base_hbm, wave_hbm, pack_ref, base_ref, head_ref, w_ref, a_ref, sems):
    bins, width = w_ref.shape
    part = a_ref.shape[0] // 4
    own = a_ref.shape[1]
    core = lax.axis_index(FREQ) & 1
    blocks = [(other, side) for other in range(2) for side in range(2)]
    acts = []
    for index, (other, side) in enumerate(blocks):
        at = pl.ds(pl.multiple_of((2 * side + (core ^ other)) * part, part), part)
        to = slice(index * part, (index + 1) * part)
        acts.append(pltpu.make_async_copy(a_hbm.at[at], a_ref.at[to], sems.at[3 + index]))
    copies = [
        pltpu.make_async_copy(wave_hbm.at[0 : head_ref.shape[0]], head_ref, sems.at[0]),
        pltpu.make_async_copy(w_hbm, w_ref, sems.at[1]),
        pltpu.make_async_copy(base_hbm, base_ref, sems.at[2]),
    ]
    for copy in acts + copies:
        copy.start()
    for index, (other, side) in enumerate(blocks):
        acts[index].wait()
        to = slice(index * part, (index + 1) * part)
        cols = slice(width + other * own, width + (other + 1) * own)
        pack_ref[side * part : (side + 1) * part, cols] = a_ref[to, :].astype(BF16)
    copies[1].wait()
    w = w_ref[...]
    pack_ref[0:bins, 0:width] = w.astype(BF16)
    pack_ref[bins : bins + AUX, 0:width] = split_rows(jnp.sum(w, axis=0, keepdims=True))
    pack_ref[bins : bins + AUX, width:] = jnp.zeros((AUX, 2 * own), BF16)
    copies[0].wait()
    copies[2].wait()


def take_heads(own_ref, side_ref, both_ref, first_ref):
    tiles = own_ref.shape[0]
    side = lax.shift_right_logical(lax.axis_index(FREQ), 1)
    own, other = own_ref[...], side_ref[0:tiles, :]
    both_ref[0:tiles, :] = own
    both_ref[tiles : 2 * tiles, :] = other
    first_ref[...] = jnp.where(side == 0, own, other)


def join_packs(own_ref, side_ref, out_ref):
    rows, packed = own_ref.shape
    quarter = packed - out_ref.shape[1]
    width = packed - 2 * quarter
    for index, pack in enumerate((own_ref, side_ref)):
        at = slice(index * rows, (index + 1) * rows)
        out_ref[at, 0:width] = pack[:, 0:width]
        out_ref[at, width:] = pack[:, width + quarter :]


def build_table(base_ref, out_ref, *, step, block):
    coarse = out_ref.shape[0] // step
    place = lax.axis_index(FREQ)
    for turn in range(4):
        for part in range(0, block, LANES):
            cols = pl.ds(pl.multiple_of((place ^ turn) * block + part, LANES), LANES)
            c2 = base_ref[2 * coarse : 2 * coarse + step, cols]
            s2 = base_ref[2 * coarse + step : 2 * coarse + 2 * step, cols]
            cos_at = slice(turn * 2 * block + part, turn * 2 * block + part + LANES)
            sin_at = slice(cos_at.start + block, cos_at.stop + block)
            for n in range(coarse):
                c1 = base_ref[n : n + 1, cols]
                s1 = base_ref[coarse + n : coarse + n + 1, cols]
                rows = slice(n * step, (n + 1) * step)
                out_ref[rows, cos_at] = (c1 * c2 - s1 * s2).astype(BF16)
                out_ref[rows, sin_at] = (-(s1 * c2 + c1 * s2)).astype(BF16)


def cut_frames(
    own_starts, side_starts, own_wave, side_wave, heads_ref, *rest, segment, last,
):
    next_ref = rest[0] if last else None
    window_ref, out_ref, ext_ref, raw_ref = rest[-4:]
    tiles = window_ref.shape[0]
    count = own_starts.shape[0]
    wave_rows = own_wave.shape[0]
    place = lax.axis_index(FREQ)
    core, side = place & 1, lax.shift_right_logical(place, 1)
    mine = side == last
    ext_ref[0:wave_rows, :] = jnp.where(mine, own_wave[...], side_wave[...])
    own_head, side_head = heads_ref[0:tiles, :], heads_ref[tiles : 2 * tiles, :]
    same = jnp.where(mine, own_head, side_head)
    after = next_ref[...] if last else jnp.where(mine, side_head, own_head)
    ext_ref[wave_rows : wave_rows + tiles, :] = jnp.where(core == 0, same, after)
    lane = lax.broadcasted_iota(jnp.int32, (tiles, LANES), 1)
    window = window_ref[...]

    def body(i, carry):
        start = jnp.where(mine, own_starts[i], side_starts[i])
        start = start & (segment - 1) if segment & (segment - 1) == 0 else lax.rem(start, segment)
        row = lax.shift_right_logical(start, 7)
        shift = start & (LANES - 1)
        back = (LANES - shift) & (LANES - 1)
        first = pltpu.roll(ext_ref[pl.ds(row, tiles), :], back, 1)
        second = pltpu.roll(ext_ref[pl.ds(row + 1, tiles), :], back, 1)
        raw_ref[pl.ds(i, tiles, stride=count), :] = jnp.where(lane < LANES - shift, first, second) * window
        return carry

    lax.fori_loop(0, count, body, 0, unroll=32)
    half = tiles // 2
    for j in range(tiles):
        rows = slice((j // half) * count, (j // half + 1) * count)
        cols = slice((j % half) * LANES, (j % half + 1) * LANES)
        out_ref[rows, cols] = raw_ref[j * count : (j + 1) * count, :].astype(BF16)


def transform(front_ref, back_ref, table_ref, energy_ref, *rest, first):
    turned_ref, frames_ref = rest if len(rest) == 2 else (None, rest[0])
    per = front_ref.shape[0] // 2
    count = 2 * per
    for part in range(2):
        rows = slice(part * per, (part + 1) * per)
        frames_ref[part * count : part * count + per, :] = front_ref[rows, :]
        frames_ref[part * count + per : (part + 1) * count, :] = back_ref[rows, :]
    block = energy_ref.shape[1] // 2
    parity = lax.broadcasted_iota(jnp.int32, (1, 2 * block), 1) & 1
    sign = 1.0 - 2.0 * parity.astype(F32)
    for index in range(2):
        at = (first + index) * 2 * block
        both = dot(frames_ref[...], table_ref[:, at : at + 2 * block])
        whole = both[:count] + sign * both[count:]
        energy = (whole[:, :block] ** 2 + whole[:, block:] ** 2) * 0.25
        energy_ref[:, index * block : (index + 1) * block] = energy
        if turned_ref is not None:
            turned_ref[index * block : (index + 1) * block, :] = energy.T


def numerators(half_acts, energy_ref, templates, numerator=None, block=0):
    block = block or energy_ref.shape[1] // 2
    for index in range(templates.shape[0] // block):
        at = slice(index * block, (index + 1) * block)
        w = templates[at, :]
        ratios = (energy_ref[:, at] / dot(half_acts, w, NT)).astype(BF16)
        term = dot(ratios, w)
        numerator = term if numerator is None else numerator + term
    return numerator


def template_share(half_acts, turned_ref, w):
    ratios = (turned_ref[...] / dot(w, half_acts, NT)).astype(BF16)
    return dot(ratios, half_acts)


def finish_acts(acts, numerator, mass, turned_ref, w, send_ref, acts_ref, total_ref):
    block = w.shape[0]
    acts = acts * numerator / mass
    acts_ref[...] = acts
    half_acts = acts.astype(BF16)
    total = jnp.sum(half_acts.astype(F32), axis=0, keepdims=True)
    total_ref[...] = jnp.broadcast_to(total, total_ref.shape)
    send_ref[block : block + AUX, :] = split_rows(total)
    send_ref[0:block, :] = template_share(half_acts, turned_ref.at[block:], w).astype(BF16)


def own_share(acts_ref, turned_ref, w_ref, own_ref):
    block = own_ref.shape[0]
    own_ref[...] = template_share(acts_ref[...].astype(BF16), turned_ref.at[0:block], w_ref[0:block, :])


def own_acts(acts_ref, keep_ref, give_ref):
    quarter = keep_ref.shape[1]
    place = lax.axis_index(FREQ)
    keep_ref[...] = acts_ref[:, pl.ds(pl.multiple_of(place * quarter, LANES), quarter)]
    give_ref[...] = acts_ref[:, pl.ds(pl.multiple_of((place ^ 1) * quarter, LANES), quarter)]


def first_update(
    energy_ref, later_ref, turned_ref, own_pack, side_pack, other_pack,
    send_ref, acts_ref, total_ref, own_w_ref, w_ref, a_ref,
):
    block = energy_ref.shape[1] // 2
    width = w_ref.shape[1]
    quarter = width // 4
    count = a_ref.shape[0]
    pitch = block + AUX
    place = lax.axis_index(FREQ)
    mass = None
    for turn, (pack, base) in enumerate(((own_pack, 0), (other_pack, 0), (side_pack, 0), (other_pack, pitch))):
        w_ref[turn * block : (turn + 1) * block, :] = pack[base : base + block, 0:width]
        part = join_rows(pack[base + block : base + pitch, 0:width])
        mass = part if mass is None else mass + part
        cols = pl.ds(pl.multiple_of((place ^ turn) * quarter, LANES), quarter)
        a_ref[:, cols] = pack[base : base + count, width : width + quarter].astype(F32)
    acts = a_ref[...]
    half_acts = acts.astype(BF16)
    numerator = numerators(half_acts, energy_ref, w_ref.at[0 : 2 * block])
    numerator = numerators(half_acts, later_ref, w_ref.at[2 * block :], numerator)
    own_w_ref[...] = w_ref[0:block, :]
    finish_acts(acts, numerator, mass, turned_ref, w_ref[block : 2 * block, :], send_ref, acts_ref, total_ref)


def tm_bit(bit):
    return lax.shift_right_logical(lax.axis_index(TM), bit) & 1


def group_rows(chain, mine, quarter):
    bit = tm_bit(chain)
    return pl.ds(pl.multiple_of(2 * chain * quarter + (bit if mine else 1 - bit) * quarter, AUX), quarter)


def unpack_templates(pieces, w_ref):
    block = 2 * w_ref.shape[0] // len(pieces)
    width = w_ref.shape[1]
    lanes = width // LANES
    rows = block // 4
    pitch = lanes * rows + AUX
    mass = None
    for index, piece in enumerate(pieces):
        turn, mine = index // 2, index % 2 == 0
        for chain in range(2):
            at = group_rows(chain, mine, rows)
            at = pl.ds(pl.multiple_of(turn * block + at.start, AUX), rows)
            base = chain * pitch
            for lane in range(lanes):
                value = piece[base + lane * rows : base + (lane + 1) * rows, :]
                w_ref[at, lane * LANES : (lane + 1) * LANES] = value
            part = join_stack(piece[base + lanes * rows : base + pitch, :], lanes)
            mass = part if mass is None else mass + part
    return jnp.concatenate([mass[lane : lane + 1, :] for lane in range(lanes)], axis=1)


def early_update(energy_ref, a_ref, mine_ref, others_ref, core_ref, w_ref, numerator_ref, mass_ref):
    size = mine_ref.shape[0]
    pieces = mine_ref, others_ref, core_ref.at[0:size], core_ref.at[size:]
    mass_ref[...] = jnp.broadcast_to(unpack_templates(pieces, w_ref), mass_ref.shape)
    numerator_ref[...] = numerators(a_ref[...].astype(BF16), energy_ref, w_ref)


def middle_update(energy_ref, a_ref, numerator_ref, mass_ref, mine_ref, others_ref, more_ref, more_mass, w_ref):
    more_mass[...] = mass_ref[...] + unpack_templates((mine_ref, others_ref), w_ref)
    more_ref[...] = numerators(a_ref[...].astype(BF16), energy_ref, w_ref, numerator_ref[...])


def later_update(
    energy_ref, turned_ref, a_ref, early_ref, numerator_ref, mass_ref, mine_ref, others_ref,
    send_ref, acts_ref, total_ref, w_ref,
):
    block = w_ref.shape[0]
    mass = mass_ref[0:1, :] + unpack_templates((mine_ref, others_ref), w_ref)
    acts = a_ref[...]
    numerator = numerators(acts.astype(BF16), energy_ref.at[:, block:], w_ref, numerator_ref[...], block)
    finish_acts(acts, numerator, mass, turned_ref, early_ref[block:, :], send_ref, acts_ref, total_ref)


def add_core(own_ref, total_ref, got_ref, keep_a, keep_b, send_a, send_b):
    block, width = own_ref.shape
    rows = block // 4
    lanes = width // LANES
    for chain, (keep, send) in enumerate(((keep_a, send_a), (keep_b, send_b))):
        for ref, mine in ((keep, True), (send, False)):
            at = group_rows(chain, mine, rows)
            for lane in range(lanes):
                cols = slice(lane * LANES, (lane + 1) * LANES)
                value = own_ref[at, cols] + got_ref[at, cols].astype(F32)
                ref[lane * rows : (lane + 1) * rows, :] = value.astype(ref.dtype)
    total = stack_lanes(total_ref[0:1, :] + join_rows(got_ref[block : block + AUX, :]))
    aux = split_stack(total)
    keep_a[lanes * rows :, :] = aux.astype(F32)
    send_a[lanes * rows :, :] = aux


def add_blocks(mine, got, lanes):
    size = mine.shape[0] - AUX if lanes else mine.shape[0]
    total = mine[0:size, :].astype(F32) + got[0:size, :].astype(F32)
    if not lanes:
        return total, None
    return total, join_stack(mine[size:, :], lanes) + join_stack(got[size:, :], lanes)


def add_pair(mine_ref, got_ref, out_ref, *, lanes):
    total, aux = add_blocks(mine_ref, got_ref, lanes)
    out_ref[0 : total.shape[0], :] = total.astype(BF16)
    if lanes:
        out_ref[total.shape[0] :, :] = split_stack(aux)


def add_chains(a_ref, got_a, b_ref, got_b, out_ref, *, lanes):
    a, aux = add_blocks(a_ref, got_a, lanes)
    b, _ = add_blocks(b_ref, got_b, 0)
    size = b.shape[0]
    out_ref[0:size, :] = a.astype(BF16)
    out_ref[size : 2 * size, :] = b.astype(BF16)
    out_ref[2 * size :, :] = split_stack(aux)


def first_templates(w_ref, mine_ref, got_ref, new_a, new_b, send_a, send_b, both_ref):
    block, width = w_ref.shape
    rows = block // 4
    lanes = width // LANES
    size = lanes * rows
    numerator, total = add_blocks(mine_ref, got_ref, lanes)
    for chain, (new, send) in enumerate(((new_a, send_a), (new_b, send_b))):
        sums = []
        for lane in range(lanes):
            old = w_ref[group_rows(chain, True, rows), lane * LANES : (lane + 1) * LANES]
            at = slice(lane * rows, (lane + 1) * rows)
            value = old * numerator[chain * size + at.start : chain * size + at.stop] / total[lane : lane + 1, :]
            new[at, :] = value
            send[at, :] = value.astype(BF16)
            sums.append(jnp.sum(value, axis=0, keepdims=True))
        send[size:, :] = split_stack(jnp.concatenate(sums, axis=0))
        both_ref[chain * (size + AUX) : (chain + 1) * (size + AUX), :] = send[...]


def last_templates(old_a, old_b, mine_ref, got_ref, new_a, new_b, *, lanes):
    numerator, total = add_blocks(mine_ref, got_ref, lanes)
    size = old_a.shape[0]
    rows = size // lanes
    for chain, (old, new) in enumerate(((old_a, new_a), (old_b, new_b))):
        for lane in range(lanes):
            at = slice(lane * rows, (lane + 1) * rows)
            value = numerator[chain * size + at.start : chain * size + at.stop]
            new[at, :] = old[at, :] * value / total[lane : lane + 1, :]


def join_groups(mine_ref, a_ref, b_ref, others_ref, all_ref):
    size = a_ref.shape[0]
    for index, ref in enumerate((a_ref, b_ref)):
        others_ref[index * size : (index + 1) * size, :] = ref[...]
        all_ref[(2 + index) * size : (3 + index) * size, :] = ref[...]
    all_ref[0 : 2 * size, :] = mine_ref[...]


def place_acts(keep_ref, given_ref, first_ref, a_out):
    part = keep_ref.shape[0] // 2
    core = lax.axis_index(FREQ) & 1
    for side in range(2):
        rows = slice(side * part, (side + 1) * part)
        for value, which in ((keep_ref, core), (given_ref, 1 - core)):
            at = pl.ds(pl.multiple_of((2 * side + which) * part, part), part)
            first = first_ref[at, :]
            a_out[at, :] = value[rows, :] * (first / first.astype(BF16).astype(F32))


def place_templates(mine_a, mine_b, got_a, got_b, w_out):
    rows = w_out.shape[0] // 4
    for chain, (mine, got) in enumerate(((mine_a, got_a), (mine_b, got_b))):
        for ref, own in ((mine, True), (got, False)):
            for lane in range(w_out.shape[1] // LANES):
                cols = slice(lane * LANES, (lane + 1) * LANES)
                w_out[group_rows(chain, own, rows), cols] = ref[lane * rows : (lane + 1) * rows, :]


def swap(block, axis, bit):
    return lax.ppermute(block, axis, [(i, i ^ bit) for i in range(lax.axis_size(axis))])


def shards(waveform, starts, templates, activations):
    tm, freq = lax.axis_size(TM), lax.axis_size(FREQ)
    block, width = templates.shape
    count = activations.shape[0] // 2
    bins = block * freq
    segment = waveform.shape[0]
    per = starts.shape[0]
    quarter = activations.shape[1]
    length = 2048
    tiles = length // LANES
    step = 32
    assert freq == 4 and tm >= 8 and tm & (tm - 1) == 0

    wave = waveform.reshape(segment // LANES, LANES)
    side_wave = swap(wave, FREQ, 2)
    side_starts = swap(starts, FREQ, 2)

    base = jnp.asarray(angle_tables(length, bins, step))
    pitch = block + AUX
    pack, base, head = call(
        prepare,
        (shape(pitch, width + 2 * quarter, BF16), shape(*base.shape, F32), shape(tiles, LANES, F32)),
        *(pltpu.with_memory_space_constraint(x, pltpu.HBM) for x in (templates, activations, base, wave)),
        in_specs=[HBM] * 4,
        scratch=[pltpu.VMEM(templates.shape, F32), pltpu.VMEM(activations.shape, F32), pltpu.SemaphoreType.DMA((7,))],
    )
    pack_y = swap(pack, FREQ, 2)
    table = call(
        functools.partial(build_table, step=step, block=block),
        shape(length // 2, 2 * bins, BF16), base, flops=4 << 20, nbytes=8 << 20,
    )
    heads, first = call(
        take_heads, (shape(2 * tiles, LANES, F32), shape(tiles, LANES, F32)), head, side_wave,
    )
    heads = swap(heads, FREQ, 1)
    route = [((t + 1) * freq + f, t * freq + f + 1) for t in range(tm - 1) for f in range(0, freq, 2)]
    following = lax.ppermute(first, (TM, FREQ), route)
    joined = call(join_packs, shape(2 * pitch, width + quarter, BF16), pack, pack_y)
    joined = swap(joined, FREQ, 1)

    window = jnp.asarray(hann_rows(length))
    frames = []
    for last in range(2):
        follow = (following,) if last else ()
        frames.append(
            call(
                functools.partial(cut_frames, segment=segment, last=last), shape(2 * per, length // 2, BF16),
                starts, side_starts, wave, side_wave, heads, *follow, window,
                in_specs=[SMEM] * 2 + [VMEM] * (4 + last),
                scratch=[
                    pltpu.VMEM((segment // LANES + tiles, LANES), F32), pltpu.VMEM((tiles * per, LANES), F32),
                ],
                nbytes=4 << 20,
            )
        )
    energies = []
    for index in range(2):
        more = (shape(2 * block, count, F32),) if index == 0 else ()
        energies += call(
            functools.partial(transform, first=2 * index), (shape(count, 2 * block, F32),) + more,
            *frames, table, scratch=[pltpu.VMEM((2 * count, length // 2), BF16)],
            flops=2 * count * length * bins, nbytes=8 << 20,
        )
    energy, turned, later_energy = energies

    outs = (shape(block + AUX, width, BF16), shape(count, width, F32), shape(8, width, F32))
    work = 3 * 2 * count * bins * width
    acts = pieces = None
    lanes = width // LANES
    size = lanes * block // 4
    for iteration in range(ITERS):
        if iteration == 0:
            send, acts, total, weights = call(
                first_update, outs + (shape(block, width, BF16),), energy, later_energy, turned, pack, pack_y, joined,
                scratch=[pltpu.VMEM((bins, width), BF16), pltpu.VMEM((count, width), F32)], flops=work,
                nbytes=4 << 20,
            )
        else:
            sums = shape(count, width, F32), shape(8, width, F32)
            weights, numerator, mass = call(
                early_update, (shape(2 * block, width, BF16),) + sums, energy, acts, *pieces[:3],
                flops=work // 3,
            )
            numerator, mass = call(
                middle_update, sums, later_energy, acts, numerator, mass, *pieces[3:5],
                scratch=[pltpu.VMEM((block, width), BF16)], flops=work // 6,
            )
            send, acts, total = call(
                later_update, outs, later_energy, turned, acts, weights, numerator, mass, *pieces[5:],
                scratch=[pltpu.VMEM((block, width), BF16)], flops=work // 2, nbytes=4 << 20,
            )
        got = swap(send, FREQ, 1)
        own = call(own_share, shape(block, width, F32), acts, turned, weights, flops=work // 6)
        if iteration == ITERS - 1:
            keep_acts, give_acts = call(own_acts, (shape(count, quarter, F32),) * 2, acts)
            given = swap(give_acts, FREQ, 1)
        sent = shape(size + AUX, LANES, BF16), shape(size, LANES, BF16)
        keep_a, keep_b, send_a, send_b = call(
            add_core, (shape(size + AUX, LANES, F32), shape(size, LANES, F32)) + sent, own, total, got,
        )
        got_a, got_b = swap(send_a, TM, 1), swap(send_b, TM, 2)
        send_a = call(functools.partial(add_pair, lanes=lanes), sent[0], keep_a, got_a)
        send_b = call(functools.partial(add_pair, lanes=0), sent[1], keep_b, got_b)
        got_a, got_b = swap(send_a, TM, 2), swap(send_b, TM, 1)
        both = shape(2 * size + AUX, LANES, BF16)
        mine = call(functools.partial(add_chains, lanes=lanes), both, send_a, got_a, send_b, got_b)
        bit = 4
        while bit < tm:
            if bit > 4:
                mine = call(functools.partial(add_pair, lanes=lanes), both, mine, got)
            got = swap(mine, TM, bit)
            bit *= 2
        part = shape(size, LANES, F32)
        if iteration < ITERS - 1:
            kept_a, kept_b, send_a, send_b, pieces = call(
                first_templates,
                (part, part, sent[0], sent[0], shape(2 * (size + AUX), LANES, BF16)), templates, mine, got,
            )
            other_a, other_b = swap(send_a, TM, 1), swap(send_b, TM, 2)
            pair = shape(2 * (size + AUX), LANES, BF16), shape(4 * (size + AUX), LANES, BF16)
            others, both_groups = call(join_groups, pair, pieces, other_a, other_b)
            in_y = [swap(pieces, FREQ, 2)]
            in_y.append(swap(others, FREQ, 2))
            in_core = swap(both_groups, FREQ, 1)
            pieces = [pieces, others, in_core] + in_y
            pieces.append(swap(in_y[0], FREQ, 1))
            pieces.append(swap(in_y[1], FREQ, 1))
        else:
            new_a, new_b = call(
                functools.partial(last_templates, lanes=lanes), (part, part), kept_a, kept_b, mine, got,
            )
            other_a = swap(new_a, TM, 1)
            other_b = swap(new_b, TM, 2)
            acts = call(
                place_acts, shape(2 * count, quarter, F32), keep_acts, given, activations,
            )
            weights = call(
                place_templates, shape(block, width, F32), new_a, new_b, other_a, other_b,
            )
            return weights, acts


def solution(mesh):
    in_specs = (P((TM, FREQ)), P((TM, FREQ)), P(FREQ, None), P(TM, FREQ))
    out_specs = (P(FREQ, None), P(TM, FREQ))
    return jax.shard_map(shards, mesh=mesh, in_specs=in_specs, out_specs=out_specs, check_vma=False)
```

```python
import functools
import math

import jax
import jax.numpy as jnp
import numpy as np
from jax import lax
from jax.experimental import pallas as pl
from jax.experimental.pallas import tpu as pltpu
from jax.sharding import PartitionSpec as P


ITERS = 2
TM, FREQ = "tm", "freq"
LANES = 128
AUX = 16
BF16 = jnp.bfloat16
F32 = jnp.float32
VMEM = pl.BlockSpec(memory_space=pltpu.VMEM)
SMEM = pl.BlockSpec(memory_space=pltpu.SMEM)
HBM = pl.BlockSpec(memory_space=pltpu.HBM)

NT = (((1,), (1,)), ((), ()))
NN = (((1,), (0,)), ((), ()))


def dot(a, b, dims=NN):
    return lax.dot_general(a, b, dims, preferred_element_type=F32)


def split_rows(total):
    high = total.astype(BF16)
    low = (total - high.astype(F32)).astype(BF16)
    row = lax.broadcasted_iota(jnp.int32, (AUX, total.shape[1]), 0)
    rows = jnp.where(row == 0, high.astype(F32), jnp.where(row == 1, low.astype(F32), 0.0))
    return rows.astype(BF16)


def join_rows(block):
    both = block.astype(F32)
    return both[0:1, :] + both[1:2, :]


def stack_lanes(row):
    return jnp.concatenate([row[:, at : at + LANES] for at in range(0, row.shape[1], LANES)], axis=0)


def split_stack(total):
    high = total.astype(BF16).astype(F32)
    rest = jnp.zeros((AUX - 2 * total.shape[0], LANES), F32)
    return jnp.concatenate([high, total - high, rest], axis=0).astype(BF16)


def join_stack(block, lanes):
    both = block.astype(F32)
    return both[0:lanes, :] + both[lanes : 2 * lanes, :]


def call(body, out_shape, *args, in_specs=None, scratch=(), flops=0, nbytes=1 << 20, limit=40 << 20):
    return pl.pallas_call(
        body,
        out_shape=out_shape,
        in_specs=in_specs if in_specs is not None else [VMEM] * len(args),
        out_specs=jax.tree.map(lambda _: VMEM, out_shape),
        scratch_shapes=list(scratch),
        cost_estimate=pl.CostEstimate(flops=flops, bytes_accessed=nbytes, transcendentals=0),
        compiler_params=pltpu.CompilerParams(vmem_limit_bytes=limit),
    )(*args)


def shape(rows, cols, dtype):
    return jax.ShapeDtypeStruct((rows, cols), dtype)


def angle_tables(length, bins, step):
    k = np.arange(bins)[None, :]

    def angles(n):
        return (n[:, None] * k % length) * (2.0 * math.pi / length)

    coarse = angles(np.arange(length // 2 // step) * step)
    fine = angles(np.arange(step))
    return np.concatenate([np.cos(coarse), np.sin(coarse), np.cos(fine), np.sin(fine)]).astype(np.float32)


def hann_rows(length):
    window = 0.5 - 0.5 * np.cos(np.arange(length) * (2.0 * math.pi / length))
    return window.astype(np.float32).reshape(length // LANES, LANES)


def prepare(w_hbm, a_hbm, base_hbm, wave_hbm, pack_ref, base_ref, head_ref, w_ref, a_ref, sems):
    bins, width = w_ref.shape
    part = a_ref.shape[0] // 4
    own = a_ref.shape[1]
    core = lax.axis_index(FREQ) & 1
    blocks = [(other, side) for other in range(2) for side in range(2)]
    acts = []
    for index, (other, side) in enumerate(blocks):
        at = pl.ds(pl.multiple_of((2 * side + (core ^ other)) * part, part), part)
        to = slice(index * part, (index + 1) * part)
        acts.append(pltpu.make_async_copy(a_hbm.at[at], a_ref.at[to], sems.at[3 + index]))
    copies = [
        pltpu.make_async_copy(wave_hbm.at[0 : head_ref.shape[0]], head_ref, sems.at[0]),
        pltpu.make_async_copy(w_hbm, w_ref, sems.at[1]),
        pltpu.make_async_copy(base_hbm, base_ref, sems.at[2]),
    ]
    for copy in acts + copies:
        copy.start()
    for index, (other, side) in enumerate(blocks):
        acts[index].wait()
        to = slice(index * part, (index + 1) * part)
        cols = slice(width + other * own, width + (other + 1) * own)
        pack_ref[side * part : (side + 1) * part, cols] = a_ref[to, :].astype(BF16)
    copies[1].wait()
    w = w_ref[...]
    pack_ref[0:bins, 0:width] = w.astype(BF16)
    pack_ref[bins : bins + AUX, 0:width] = split_rows(jnp.sum(w, axis=0, keepdims=True))
    pack_ref[bins : bins + AUX, width:] = jnp.zeros((AUX, 2 * own), BF16)
    copies[0].wait()
    copies[2].wait()


def take_heads(own_ref, side_ref, both_ref, first_ref):
    tiles = own_ref.shape[0]
    side = lax.shift_right_logical(lax.axis_index(FREQ), 1)
    own, other = own_ref[...], side_ref[0:tiles, :]
    both_ref[0:tiles, :] = own
    both_ref[tiles : 2 * tiles, :] = other
    first_ref[...] = jnp.where(side == 0, own, other)


def join_packs(own_ref, side_ref, out_ref):
    rows, packed = own_ref.shape
    quarter = packed - out_ref.shape[1]
    width = packed - 2 * quarter
    for index, pack in enumerate((own_ref, side_ref)):
        at = slice(index * rows, (index + 1) * rows)
        out_ref[at, 0:width] = pack[:, 0:width]
        out_ref[at, width:] = pack[:, width + quarter :]


def build_table(base_ref, out_ref, *, step, block):
    coarse = out_ref.shape[0] // step
    place = lax.axis_index(FREQ)
    for turn in range(4):
        for part in range(0, block, LANES):
            cols = pl.ds(pl.multiple_of((place ^ turn) * block + part, LANES), LANES)
            c2 = base_ref[2 * coarse : 2 * coarse + step, cols]
            s2 = base_ref[2 * coarse + step : 2 * coarse + 2 * step, cols]
            cos_at = slice(turn * 2 * block + part, turn * 2 * block + part + LANES)
            sin_at = slice(cos_at.start + block, cos_at.stop + block)
            for n in range(coarse):
                c1 = base_ref[n : n + 1, cols]
                s1 = base_ref[coarse + n : coarse + n + 1, cols]
                rows = slice(n * step, (n + 1) * step)
                out_ref[rows, cos_at] = (c1 * c2 - s1 * s2).astype(BF16)
                out_ref[rows, sin_at] = (-(s1 * c2 + c1 * s2)).astype(BF16)


def cut_frames(
    own_starts, side_starts, own_wave, side_wave, heads_ref, *rest, segment, last,
):
    next_ref = rest[0] if last else None
    window_ref, out_ref, ext_ref, raw_ref = rest[-4:]
    tiles = window_ref.shape[0]
    count = own_starts.shape[0]
    wave_rows = own_wave.shape[0]
    place = lax.axis_index(FREQ)
    core, side = place & 1, lax.shift_right_logical(place, 1)
    mine = side == last
    ext_ref[0:wave_rows, :] = jnp.where(mine, own_wave[...], side_wave[...])
    own_head, side_head = heads_ref[0:tiles, :], heads_ref[tiles : 2 * tiles, :]
    same = jnp.where(mine, own_head, side_head)
    after = next_ref[...] if last else jnp.where(mine, side_head, own_head)
    ext_ref[wave_rows : wave_rows + tiles, :] = jnp.where(core == 0, same, after)
    lane = lax.broadcasted_iota(jnp.int32, (tiles, LANES), 1)
    window = window_ref[...]

    def body(i, carry):
        start = jnp.where(mine, own_starts[i], side_starts[i])
        start = start & (segment - 1) if segment & (segment - 1) == 0 else lax.rem(start, segment)
        row = lax.shift_right_logical(start, 7)
        shift = start & (LANES - 1)
        back = (LANES - shift) & (LANES - 1)
        first = pltpu.roll(ext_ref[pl.ds(row, tiles), :], back, 1)
        second = pltpu.roll(ext_ref[pl.ds(row + 1, tiles), :], back, 1)
        raw_ref[pl.ds(i, tiles, stride=count), :] = jnp.where(lane < LANES - shift, first, second) * window
        return carry

    lax.fori_loop(0, count, body, 0, unroll=64)
    half = tiles // 2
    for j in range(tiles):
        rows = slice((j // half) * count, (j // half + 1) * count)
        cols = slice((j % half) * LANES, (j % half + 1) * LANES)
        out_ref[rows, cols] = raw_ref[j * count : (j + 1) * count, :].astype(BF16)


def transform(front_ref, back_ref, table_ref, energy_ref, *rest, first):
    turned_ref, frames_ref = rest if len(rest) == 2 else (None, rest[0])
    per = front_ref.shape[0] // 2
    count = 2 * per
    for part in range(2):
        rows = slice(part * per, (part + 1) * per)
        frames_ref[part * count : part * count + per, :] = front_ref[rows, :]
        frames_ref[part * count + per : (part + 1) * count, :] = back_ref[rows, :]
    block = energy_ref.shape[1] // 2
    parity = lax.broadcasted_iota(jnp.int32, (1, 2 * block), 1) & 1
    sign = 1.0 - 2.0 * parity.astype(F32)
    for index in range(2):
        at = (first + index) * 2 * block
        both = dot(frames_ref[...], table_ref[:, at : at + 2 * block])
        whole = both[:count] + sign * both[count:]
        energy = (whole[:, :block] ** 2 + whole[:, block:] ** 2) * 0.25
        energy_ref[:, index * block : (index + 1) * block] = energy
        if turned_ref is not None:
            turned_ref[index * block : (index + 1) * block, :] = energy.T


def numerators(half_acts, energy_ref, templates, numerator=None, block=0):
    block = block or energy_ref.shape[1] // 2
    for index in range(templates.shape[0] // block):
        at = slice(index * block, (index + 1) * block)
        w = templates[at, :]
        ratios = (energy_ref[:, at] / dot(half_acts, w, NT)).astype(BF16)
        term = dot(ratios, w)
        numerator = term if numerator is None else numerator + term
    return numerator


def template_share(half_acts, turned_ref, w):
    ratios = (turned_ref[...] / dot(w, half_acts, NT)).astype(BF16)
    return dot(ratios, half_acts)


def finish_acts(acts, numerator, mass, turned_ref, w, send_ref, acts_ref, total_ref):
    block = w.shape[0]
    acts = acts * numerator / mass
    acts_ref[...] = acts
    half_acts = acts.astype(BF16)
    total = jnp.sum(half_acts.astype(F32), axis=0, keepdims=True)
    total_ref[...] = jnp.broadcast_to(total, total_ref.shape)
    send_ref[block : block + AUX, :] = split_rows(total)
    send_ref[0:block, :] = template_share(half_acts, turned_ref.at[block:], w).astype(BF16)


def own_share(acts_ref, turned_ref, w_ref, own_ref):
    block = own_ref.shape[0]
    own_ref[...] = template_share(acts_ref[...].astype(BF16), turned_ref.at[0:block], w_ref[0:block, :])


def own_acts(acts_ref, keep_ref, give_ref):
    quarter = keep_ref.shape[1]
    place = lax.axis_index(FREQ)
    keep_ref[...] = acts_ref[:, pl.ds(pl.multiple_of(place * quarter, LANES), quarter)]
    give_ref[...] = acts_ref[:, pl.ds(pl.multiple_of((place ^ 1) * quarter, LANES), quarter)]


def first_update(
    energy_ref, later_ref, turned_ref, own_pack, side_pack, other_pack,
    send_ref, acts_ref, total_ref, own_w_ref, w_ref, a_ref,
):
    block = energy_ref.shape[1] // 2
    width = w_ref.shape[1]
    quarter = width // 4
    count = a_ref.shape[0]
    pitch = block + AUX
    place = lax.axis_index(FREQ)
    mass = None
    for turn, (pack, base) in enumerate(((own_pack, 0), (other_pack, 0), (side_pack, 0), (other_pack, pitch))):
        w_ref[turn * block : (turn + 1) * block, :] = pack[base : base + block, 0:width]
        part = join_rows(pack[base + block : base + pitch, 0:width])
        mass = part if mass is None else mass + part
        cols = pl.ds(pl.multiple_of((place ^ turn) * quarter, LANES), quarter)
        a_ref[:, cols] = pack[base : base + count, width : width + quarter].astype(F32)
    acts = a_ref[...]
    half_acts = acts.astype(BF16)
    numerator = numerators(half_acts, energy_ref, w_ref.at[0 : 2 * block])
    numerator = numerators(half_acts, later_ref, w_ref.at[2 * block :], numerator)
    own_w_ref[...] = w_ref[0:block, :]
    finish_acts(acts, numerator, mass, turned_ref, w_ref[block : 2 * block, :], send_ref, acts_ref, total_ref)


def tm_bit(bit):
    return lax.shift_right_logical(lax.axis_index(TM), bit) & 1


def group_rows(chain, mine, quarter):
    bit = tm_bit(chain)
    return pl.ds(pl.multiple_of(2 * chain * quarter + (bit if mine else 1 - bit) * quarter, AUX), quarter)


def unpack_templates(pieces, w_ref):
    block = 2 * w_ref.shape[0] // len(pieces)
    width = w_ref.shape[1]
    lanes = width // LANES
    rows = block // 4
    pitch = lanes * rows + AUX
    mass = None
    for index, piece in enumerate(pieces):
        turn, mine = index // 2, index % 2 == 0
        for chain in range(2):
            at = group_rows(chain, mine, rows)
            at = pl.ds(pl.multiple_of(turn * block + at.start, AUX), rows)
            base = chain * pitch
            for lane in range(lanes):
                value = piece[base + lane * rows : base + (lane + 1) * rows, :]
                w_ref[at, lane * LANES : (lane + 1) * LANES] = value
            part = join_stack(piece[base + lanes * rows : base + pitch, :], lanes)
            mass = part if mass is None else mass + part
    return jnp.concatenate([mass[lane : lane + 1, :] for lane in range(lanes)], axis=1)


def early_update(energy_ref, a_ref, mine_ref, others_ref, core_ref, w_ref, numerator_ref, mass_ref):
    size = mine_ref.shape[0]
    pieces = mine_ref, others_ref, core_ref.at[0:size], core_ref.at[size:]
    mass_ref[...] = jnp.broadcast_to(unpack_templates(pieces, w_ref), mass_ref.shape)
    numerator_ref[...] = numerators(a_ref[...].astype(BF16), energy_ref, w_ref)


def middle_update(energy_ref, a_ref, numerator_ref, mass_ref, mine_ref, others_ref, more_ref, more_mass, w_ref):
    more_mass[...] = mass_ref[...] + unpack_templates((mine_ref, others_ref), w_ref)
    more_ref[...] = numerators(a_ref[...].astype(BF16), energy_ref, w_ref, numerator_ref[...])


def later_update(
    energy_ref, turned_ref, a_ref, early_ref, numerator_ref, mass_ref, mine_ref, others_ref,
    send_ref, acts_ref, total_ref, w_ref,
):
    block = w_ref.shape[0]
    mass = mass_ref[0:1, :] + unpack_templates((mine_ref, others_ref), w_ref)
    acts = a_ref[...]
    numerator = numerators(acts.astype(BF16), energy_ref.at[:, block:], w_ref, numerator_ref[...], block)
    finish_acts(acts, numerator, mass, turned_ref, early_ref[block:, :], send_ref, acts_ref, total_ref)


def add_core(own_ref, total_ref, got_ref, keep_a, keep_b, send_a, send_b):
    block, width = own_ref.shape
    rows = block // 4
    lanes = width // LANES
    for chain, (keep, send) in enumerate(((keep_a, send_a), (keep_b, send_b))):
        for ref, mine in ((keep, True), (send, False)):
            at = group_rows(chain, mine, rows)
            for lane in range(lanes):
                cols = slice(lane * LANES, (lane + 1) * LANES)
                value = own_ref[at, cols] + got_ref[at, cols].astype(F32)
                ref[lane * rows : (lane + 1) * rows, :] = value.astype(ref.dtype)
    total = stack_lanes(total_ref[0:1, :] + join_rows(got_ref[block : block + AUX, :]))
    aux = split_stack(total)
    keep_a[lanes * rows :, :] = aux.astype(F32)
    send_a[lanes * rows :, :] = aux


def add_blocks(mine, got, lanes):
    size = mine.shape[0] - AUX if lanes else mine.shape[0]
    total = mine[0:size, :].astype(F32) + got[0:size, :].astype(F32)
    if not lanes:
        return total, None
    return total, join_stack(mine[size:, :], lanes) + join_stack(got[size:, :], lanes)


def add_pair(mine_ref, got_ref, out_ref, *, lanes):
    total, aux = add_blocks(mine_ref, got_ref, lanes)
    out_ref[0 : total.shape[0], :] = total.astype(BF16)
    if lanes:
        out_ref[total.shape[0] :, :] = split_stack(aux)


def new_rows(old, mine_ref, got_ref, total_ref, chain, lanes):
    numerator, total = add_blocks(mine_ref, got_ref, 0 if chain else lanes)
    if chain:
        total = total_ref[0:lanes, :]
    else:
        total_ref[...] = jnp.zeros_like(total_ref)
        total_ref[0:lanes, :] = total
    rows = numerator.shape[0] // lanes
    for lane in range(lanes):
        at = slice(lane * rows, (lane + 1) * rows)
        yield at, old(lane, at) * numerator[at, :] / total[lane : lane + 1, :]


def first_templates(w_ref, mine_ref, got_ref, *rest, chain, lanes):
    total_ref, new, send = rest if chain else rest[::-1]
    rows = w_ref.shape[0] // 4
    sums = []

    def old(lane, at):
        return w_ref[group_rows(chain, True, rows), lane * LANES : (lane + 1) * LANES]

    for at, value in new_rows(old, mine_ref, got_ref, total_ref, chain, lanes):
        new[at, :] = value
        send[at, :] = value.astype(BF16)
        sums.append(jnp.sum(value, axis=0, keepdims=True))
    send[lanes * rows :, :] = split_stack(jnp.concatenate(sums, axis=0))


def last_templates(old_ref, mine_ref, got_ref, *rest, chain, lanes):
    total_ref, new = rest if chain else rest[::-1]
    for at, value in new_rows(lambda lane, at: old_ref[at, :], mine_ref, got_ref, total_ref, chain, lanes):
        new[at, :] = value


def join_two(a_ref, b_ref, out_ref):
    out_ref[0 : a_ref.shape[0], :] = a_ref[...]
    out_ref[a_ref.shape[0] :, :] = b_ref[...]


def join_groups(mine_ref, a_ref, b_ref, others_ref, all_ref):
    size = a_ref.shape[0]
    for index, ref in enumerate((a_ref, b_ref)):
        others_ref[index * size : (index + 1) * size, :] = ref[...]
        all_ref[(2 + index) * size : (3 + index) * size, :] = ref[...]
    all_ref[0 : 2 * size, :] = mine_ref[...]


def place_acts(keep_ref, given_ref, first_ref, a_out):
    part = keep_ref.shape[0] // 2
    core = lax.axis_index(FREQ) & 1
    for side in range(2):
        rows = slice(side * part, (side + 1) * part)
        for value, which in ((keep_ref, core), (given_ref, 1 - core)):
            at = pl.ds(pl.multiple_of((2 * side + which) * part, part), part)
            first = first_ref[at, :]
            a_out[at, :] = value[rows, :] * (first / first.astype(BF16).astype(F32))


def place_templates(mine_a, mine_b, got_a, got_b, w_out):
    rows = w_out.shape[0] // 4
    for chain, (mine, got) in enumerate(((mine_a, got_a), (mine_b, got_b))):
        for ref, own in ((mine, True), (got, False)):
            for lane in range(w_out.shape[1] // LANES):
                cols = slice(lane * LANES, (lane + 1) * LANES)
                w_out[group_rows(chain, own, rows), cols] = ref[lane * rows : (lane + 1) * rows, :]


def swap(block, axis, bit):
    return lax.ppermute(block, axis, [(i, i ^ bit) for i in range(lax.axis_size(axis))])


def shards(waveform, starts, templates, activations):
    tm, freq = lax.axis_size(TM), lax.axis_size(FREQ)
    block, width = templates.shape
    count = activations.shape[0] // 2
    bins = block * freq
    segment = waveform.shape[0]
    per = starts.shape[0]
    quarter = activations.shape[1]
    length = 2048
    tiles = length // LANES
    step = 32
    assert freq == 4 and tm >= 8 and tm & (tm - 1) == 0

    wave = waveform.reshape(segment // LANES, LANES)
    side_wave = swap(wave, FREQ, 2)
    side_starts = swap(starts, FREQ, 2)

    base = jnp.asarray(angle_tables(length, bins, step))
    pitch = block + AUX
    pack, base, head = call(
        prepare,
        (shape(pitch, width + 2 * quarter, BF16), shape(*base.shape, F32), shape(tiles, LANES, F32)),
        *(pltpu.with_memory_space_constraint(x, pltpu.HBM) for x in (templates, activations, base, wave)),
        in_specs=[HBM] * 4,
        scratch=[pltpu.VMEM(templates.shape, F32), pltpu.VMEM(activations.shape, F32), pltpu.SemaphoreType.DMA((7,))],
    )
    pack_y = swap(pack, FREQ, 2)
    table = call(
        functools.partial(build_table, step=step, block=block),
        shape(length // 2, 2 * bins, BF16), base, flops=4 << 20, nbytes=8 << 20,
    )
    heads, first = call(
        take_heads, (shape(2 * tiles, LANES, F32), shape(tiles, LANES, F32)), head, side_wave,
    )
    heads = swap(heads, FREQ, 1)
    route = [((t + 1) * freq + f, t * freq + f + 1) for t in range(tm - 1) for f in range(0, freq, 2)]
    following = lax.ppermute(first, (TM, FREQ), route)
    joined = call(join_packs, shape(2 * pitch, width + quarter, BF16), pack, pack_y)
    joined = swap(joined, FREQ, 1)

    window = jnp.asarray(hann_rows(length))
    frames = []
    for last in range(2):
        follow = (following,) if last else ()
        frames.append(
            call(
                functools.partial(cut_frames, segment=segment, last=last), shape(2 * per, length // 2, BF16),
                starts, side_starts, wave, side_wave, heads, *follow, window,
                in_specs=[SMEM] * 2 + [VMEM] * (4 + last),
                scratch=[
                    pltpu.VMEM((segment // LANES + tiles, LANES), F32), pltpu.VMEM((tiles * per, LANES), F32),
                ],
                nbytes=4 << 20,
            )
        )
    energies = []
    for index in range(2):
        more = (shape(2 * block, count, F32),) if index == 0 else ()
        energies += call(
            functools.partial(transform, first=2 * index), (shape(count, 2 * block, F32),) + more,
            *frames, table, scratch=[pltpu.VMEM((2 * count, length // 2), BF16)],
            flops=2 * count * length * bins, nbytes=8 << 20,
        )
    energy, turned, later_energy = energies

    outs = (shape(block + AUX, width, BF16), shape(count, width, F32), shape(8, width, F32))
    work = 3 * 2 * count * bins * width
    acts = pieces = None
    lanes = width // LANES
    size = lanes * block // 4
    for iteration in range(ITERS):
        if iteration == 0:
            send, acts, total, weights = call(
                first_update, outs + (shape(block, width, BF16),), energy, later_energy, turned, pack, pack_y, joined,
                scratch=[pltpu.VMEM((bins, width), BF16), pltpu.VMEM((count, width), F32)], flops=work,
                nbytes=4 << 20,
            )
        else:
            sums = shape(count, width, F32), shape(8, width, F32)
            weights, numerator, mass = call(
                early_update, (shape(2 * block, width, BF16),) + sums, energy, acts, *pieces[:3],
                flops=work // 3,
            )
            numerator, mass = call(
                middle_update, sums, later_energy, acts, numerator, mass, *pieces[3:5],
                scratch=[pltpu.VMEM((block, width), BF16)], flops=work // 6,
            )
            send, acts, total = call(
                later_update, outs, later_energy, turned, acts, weights, numerator, mass, *pieces[5:],
                scratch=[pltpu.VMEM((block, width), BF16)], flops=work // 2, nbytes=4 << 20,
            )
        got = swap(send, FREQ, 1)
        own = call(own_share, shape(block, width, F32), acts, turned, weights, flops=work // 6)
        if iteration == ITERS - 1:
            keep_acts, give_acts = call(own_acts, (shape(count, quarter, F32),) * 2, acts)
            given = swap(give_acts, FREQ, 1)
        sent = shape(size + AUX, LANES, BF16), shape(size, LANES, BF16)
        keep_a, keep_b, send_a, send_b = call(
            add_core, (shape(size + AUX, LANES, F32), shape(size, LANES, F32)) + sent, own, total, got,
        )
        sides = []
        for keep, send, bits in ((keep_a, send_a, (1, 2)), (keep_b, send_b, (2, 1))):
            sides.append([keep, swap(send, TM, bits[0])])
        for chain, bits in enumerate(((1, 2), (2, 1))):
            aux = 0 if chain else lanes
            for bit in (bits[1],) + tuple(4 << i for i in range((tm // 4).bit_length() - 1)):
                mine = call(functools.partial(add_pair, lanes=aux), sent[chain], *sides[chain])
                sides[chain] = [mine, swap(mine, TM, bit)]
        part = shape(size, LANES, F32)
        totals = shape(8, LANES, F32)
        if iteration < ITERS - 1:
            send_a, kept_a, total = call(
                functools.partial(first_templates, chain=0, lanes=lanes), (sent[0], part, totals), templates, *sides[0],
            )
            other_a = swap(send_a, TM, 1)
            kept_b, send_b = call(
                functools.partial(first_templates, chain=1, lanes=lanes), (part, sent[0]), templates, *sides[1],
                total,
            )
            other_b = swap(send_b, TM, 2)
            pieces = call(join_two, shape(2 * (size + AUX), LANES, BF16), send_a, send_b)
            pair = shape(2 * (size + AUX), LANES, BF16), shape(4 * (size + AUX), LANES, BF16)
            others, both_groups = call(join_groups, pair, pieces, other_a, other_b)
            in_y = [swap(pieces, FREQ, 2)]
            in_y.append(swap(others, FREQ, 2))
            in_core = swap(both_groups, FREQ, 1)
            pieces = [pieces, others, in_core] + in_y
            pieces.append(swap(in_y[0], FREQ, 1))
            pieces.append(swap(in_y[1], FREQ, 1))
        else:
            new_a, total = call(
                functools.partial(last_templates, chain=0, lanes=lanes), (part, totals), kept_a, *sides[0],
            )
            other_a = swap(new_a, TM, 1)
            new_b = call(
                functools.partial(last_templates, chain=1, lanes=lanes), part, kept_b, *sides[1], total,
            )
            other_b = swap(new_b, TM, 2)
            acts = call(
                place_acts, shape(2 * count, quarter, F32), keep_acts, given, activations,
            )
            weights = call(
                place_templates, shape(block, width, F32), new_a, new_b, other_a, other_b,
            )
            return weights, acts


def solution(mesh):
    in_specs = (P((TM, FREQ)), P((TM, FREQ)), P(FREQ, None), P(TM, FREQ))
    out_specs = (P(FREQ, None), P(TM, FREQ))
    return jax.shard_map(shards, mesh=mesh, in_specs=in_specs, out_specs=out_specs, check_vma=False)
```
